32 devices in a mesh: groups: 2 (over x), ctx: 16 (over z, y, core).
Axes of the slice: x: 2, y: 2, z: 4, core: 2. Of those that a mesh axis runs over, the one named last changes fastest.
Arguments:
- queries: bfloat16 [4096, 1024], P(('groups', 'ctx')), parts along dimension 0, may hold values from -100 to 100
- encoder_rows: bfloat16 [3072, 2048], P(('groups', 'ctx')), parts along dimension 0, may hold values from -6 to 6
- key_weight: bfloat16 [2048, 1024], replicated, may hold values from -0.125 to 0.125
- value_weight: bfloat16 [2048, 1024], replicated, may hold values from -0.125 to 0.125
- out_weight: bfloat16 [1024, 2048], P(None, 'ctx'), may hold values from -0.1875 to 0.1875
Outputs:
- attended: bfloat16 [4096, 2048], P(('groups', 'ctx')), parts along dimension 0
The draws below stay inside these ranges and needn't reach their ends.
There are 2 independent parts, one for each index of `groups`. The reference program is written for one: setup_inputs(seed, part) draws one part's arguments, and reference() takes and returns one part's arrays. A program takes and returns all parts, laid end to end along the dimension named above; an argument that names none is the same for every part. Nothing has to cross between parts.
All inputs are finite; a program needn't handle non-finite values.
Results may differ from the reference program's by a relative error of at most 0.009.
The reference program's roundings to bfloat16 on the way (of `keys`, `values`, `weights` and `context`) count: a program that leaves them out, or rounds other values in their place, can miss the bound.
Values may be sent and summed in bfloat16 or wider, within the bound.
A program may use at most 192 MiB of HBM per device.

```python
import math
import jax
import jax.numpy as jnp
from jax import lax

D = 2048
HEADS = 16
DH = 64
HD = 1024
QTOK = 2048
ENC = 1536


def draw_queries(key, part):
    base = jax.random.normal(key, (QTOK, HEADS * DH), jnp.float32)
    vals = jnp.clip(base, -6.0, 6.0)
    return vals.astype(jnp.bfloat16)


def shard_levels(rng, dims, pieces, smallest, high):
    level = 1.0
    for axis_at, parts in pieces:
        draws = jax.random.uniform(jax.random.fold_in(jax.random.fold_in(rng, 6), axis_at), (parts,), jnp.float32, smallest / len(pieces), high / len(pieces))
        level = level * jnp.repeat(jnp.exp(draws), dims[axis_at] // parts).reshape((-1,) + (1,) * (len(dims) - 1 - axis_at))
    return level


def normal_values(stream_key, dims, deviation, reach, shards=(), dtype=jnp.bfloat16):
    array = deviation * jax.random.normal(stream_key, dims, jnp.float32)
    if shards:
        array = array * shard_levels(stream_key, dims, shards, -0.22, 0.18)
    return jnp.clip(array, -reach, reach).astype(dtype)


def setup_inputs(seed: int = 0, part: int = 0) -> dict:
    key_of = jax.random.split(jax.random.key(seed), 6)
    part_splits = jax.random.split(jax.random.fold_in(key_of[5], part), 6)
    return {
        "queries": draw_queries(jax.random.fold_in(jax.random.fold_in(key_of[5], part), 71), part),
        "encoder_rows": normal_values(part_splits[1], (ENC, D), 1.0, 6.0, ((0, 16),)),
        "key_weight": normal_values(key_of[2], (D, HD), D ** -0.5, 0.125),
        "value_weight": normal_values(key_of[3], (D, HD), D ** -0.5, 0.125),
        "out_weight": normal_values(key_of[4], (HD, D), HD ** -0.5, 0.1875, ((1, 16),)),
    }


def reference(queries, encoder_rows, key_weight, value_weight, out_weight):
    keys = jnp.dot(encoder_rows, key_weight, preferred_element_type=jnp.float32).astype(jnp.bfloat16)
    values = jnp.dot(encoder_rows, value_weight, preferred_element_type=jnp.float32).astype(jnp.bfloat16)
    keys3 = keys.reshape(ENC, HEADS, DH).astype(jnp.float32)
    values3 = values.reshape(ENC, HEADS, DH).astype(jnp.float32)
    block = math.gcd(QTOK, 512)
    blocks = queries.reshape(QTOK // block, block, HEADS, DH)

    def attend(query_block):
        scores = jnp.einsum("qhd,khd->hqk", query_block.astype(jnp.float32), keys3) * 0.125
        top = jnp.max(scores, axis=-1)
        expo = jnp.exp(scores - top[..., None])
        total = jnp.sum(expo, axis=-1)
        weights = expo.astype(jnp.bfloat16).astype(jnp.float32)
        summed = jnp.einsum("hqk,khd->qhd", weights, values3)
        context = (summed / jnp.transpose(total)[:, :, None]).astype(jnp.bfloat16).reshape(block, HD)
        return jnp.dot(context, out_weight, preferred_element_type=jnp.float32).astype(jnp.bfloat16)

    return lax.map(attend, blocks).reshape(QTOK, D)
```

```python
import functools
import math

import jax
import jax.numpy as jnp
from jax import lax
from jax.experimental import pallas as pl
from jax.experimental.pallas import tpu as pltpu
from jax.sharding import PartitionSpec as P

HEADS = 16
DH = 64
PAIR = 2 * DH
MESH = pl.DeviceIdType.MESH
LOG2E = 1.4426950408889634
SPLIT = 2


def kernel(
    groups, n, plane, chunks,
    q_hbm, e_hbm, kw_hbm, vw_hbm, ow_ref, o_ref,
    q_ref, e_ref, kw, vw, qpack, kvpack, qall, kvall, cpack, call, ctx, wall,
    load_sem, own_sem, in_sem, q_send, q_recv, kv_send, kv_recv, c_send, c_recv,
    z_send, z_recv, y_send, y_recv, x_send, x_recv, b_send, b_recv,
):
    grp = lax.axis_index("groups")
    me = lax.axis_index("ctx")
    rows = q_ref.shape[0]
    enc = e_ref.shape[0]
    depth = ow_ref.shape[0]
    copies = n // HEADS
    share = rows // copies
    half = share // 2
    part = depth // groups
    layers = n // plane
    zed = me // plane
    spot = me % plane
    far = plane // 2
    over = zed * plane + (spot + far) % plane
    mate = zed * plane + (spot // 2) * 2 + (1 - spot % 2)

    def loads(j):
        width = kw.shape[2]
        cols = pl.ds(j * width, width)
        return (
            pltpu.make_async_copy(kw_hbm.at[:, cols], kw.at[j], load_sem.at[j]),
            pltpu.make_async_copy(vw_hbm.at[:, cols], vw.at[j], load_sem.at[chunks + j]),
        )

    barrier = pltpu.get_barrier_semaphore()

    def greet(i, carry):
        pl.semaphore_signal(
            barrier, inc=1, device_id=(grp, (me + i) % n), device_id_type=MESH
        )
        return carry

    lax.fori_loop(1, n, greet, 0)
    for g in range(1, groups):
        pl.semaphore_signal(
            barrier, inc=1, device_id=((grp + g) % groups, me), device_id_type=MESH
        )

    take_q = pltpu.make_async_copy(q_hbm, q_ref, in_sem.at[0])
    take_e = pltpu.make_async_copy(e_hbm, e_ref, in_sem.at[1])
    own = pltpu.make_async_copy(ow_ref, wall.at[me], own_sem)
    take_q.start()
    take_e.start()
    for copy in loads(0):
        copy.start()
    own.start()
    for j in range(1, chunks):
        for copy in loads(j):
            copy.start()

    take_q.wait()
    for d in range(n):
        r0, c0 = (d // HEADS) * share, (d % HEADS) * DH
        qpack[d] = jnp.concatenate(
            [q_ref[r0 : r0 + half, c0 : c0 + DH], q_ref[r0 + half : r0 + share, c0 : c0 + DH]],
            axis=1,
        )
    def remote(src, dst, send, recv, to):
        return pltpu.make_async_remote_copy(
            src_ref=src, dst_ref=dst, send_sem=send, recv_sem=recv,
            device_id=to, device_id_type=MESH,
        )

    def q_copy(d, s):
        return remote(qpack.at[d], qall.at[s], q_send.at[d], q_recv.at[s], (grp, d))

    def kv_copy(d, s):
        return remote(
            kvpack.at[d % HEADS], kvall.at[pl.ds(s * enc, enc)],
            kv_send.at[d], kv_recv.at[s], (grp, d),
        )

    def c_copy(d, s):
        return remote(cpack.at[d], call.at[s], c_send.at[d], c_recv.at[s], (grp, d))

    split = SPLIT
    piece = part // split

    def rows_of(whose, p):
        return pl.ds(whose * part + p * piece, piece)

    def z_copy(src, way, p):
        block = wall.at[src * plane + spot, rows_of(grp, p)]
        to = zed + 1 - 2 * way
        return remote(
            block, block, z_send.at[(way * layers + src) * split + p], z_recv.at[src * split + p],
            (grp, to * plane + spot),
        )

    def hop(src, way, p, act):
        @pl.when((zed > 0) if way else (zed + 1 < layers))
        def _():
            act(z_copy(src, way, p))

    def y_copy(layer, at, to, p):
        block = wall.at[layer * plane + at, rows_of(grp, p)]
        slot = layer * split + p
        return remote(block, block, y_send.at[slot], y_recv.at[slot], (grp, to))

    def near_copy(at, to):
        block = wall.at[zed * plane + at]
        slot = zed * split
        return remote(block, block, y_send.at[slot], y_recv.at[slot], (grp, to))

    def x_copy(layer, side, g, whose, p):
        at = layer * plane + (spot + side * far) % plane
        block = wall.at[at, rows_of(whose, p)]
        slot = ((g * 2 + side) * layers + layer) * split + p
        return remote(
            block, block, x_send.at[slot], x_recv.at[slot], ((grp + g) % groups, me)
        )

    def b_copy(layer, side, at):
        block = wall.at[layer * plane + (at + side * far) % plane]
        slot = side * layers + layer
        return remote(block, block, b_send.at[slot], b_recv.at[slot], (grp, mate))

    def some(first, last, body):
        def step(i, carry):
            body((me + i) % n)
            return carry

        lax.fori_loop(first, last, step, 0)

    def others(body):
        some(1, n, body)

    def beyond(body):
        def step(i, carry):
            body((zed + i) % layers)
            return carry

        lax.fori_loop(1, layers, step, 0)

    def begin():
        own.wait()
        pl.semaphore_wait(barrier, n - 1 + groups - 1)
        for p in range(split):
            hop(zed, 0, p, lambda copy: copy.start())
            hop(zed, 1, p, lambda copy: copy.start())
        near_copy(spot, over).start()
        b_copy(zed, 0, spot).start()

    begin()
    take_e.wait()
    heads = HEADS // chunks
    for j in range(chunks):
        one, two = loads(j)
        one.wait()
        two.wait()
        keys = jnp.dot(e_ref[...], kw[j], preferred_element_type=jnp.float32).astype(jnp.bfloat16)
        values = jnp.dot(e_ref[...], vw[j], preferred_element_type=jnp.float32).astype(jnp.bfloat16)
        for h in range(heads):
            cols = slice(h * DH, (h + 1) * DH)
            kvpack[j * heads + h] = jnp.concatenate([keys[:, cols], values[:, cols]], axis=1)

    def sources(k, body):
        for way in range(2):
            src = zed + k if way else zed - k

            @pl.when((src < layers) if way else (src >= 0))
            def _():
                body(src, way)

    def send_x(z, side, p):
        for g in range(1, groups):
            x_copy(z, side, g, grp, p).start()

    def take_x(z, side):
        for g in range(1, groups):
            for p in range(split):
                x_copy(z, side, g, (grp + groups - g) % groups, p).wait_recv()
        b_copy(z, side, spot).start()

    def pass_on(src, way):
        for p in range(split):
            z_copy(src, way, p).wait_recv()
            hop(src, way, p, lambda copy: copy.start())
            y_copy(src, spot, over, p).start()
            send_x(src, 0, p)

    def pass_x(z, way):
        for p in range(split):
            y_copy(z, (spot + far) % plane, over, p).wait_recv()
            send_x(z, 1, p)

    def pass_b(z, way):
        take_x(z, 0)
        take_x(z, 1)

    def pass_near():
        near_copy((spot + far) % plane, over).wait_recv()
        b_copy(zed, 1, spot).start()

    steps = layers - 1
    def bound(k):
        return n - (n - 1) * (steps - k) * (steps - k) // (steps * steps)

    for k in range(1, steps):
        some(bound(k - 1), bound(k), lambda d: kv_copy(d, me).start())
        sources(k, pass_on)
        if k == 1:
            pass_near()
        else:
            sources(k - 1, pass_x)
    some(bound(steps - 1), n, lambda d: kv_copy(d, me).start())
    others(lambda d: q_copy(d, me).start())
    sources(steps - 1, pass_x)
    sources(steps, pass_on)
    kvall[pl.ds(me * enc, enc)] = kvpack[me % HEADS]
    qall[me] = qpack[me]
    others(lambda s: kv_copy(s, s).wait_recv())

    together = 2

    def attend(i, carry):
        whose = [(me + 1 + i * together + j) % n for j in range(together)]
        pieces = []
        for s in whose:

            @pl.when(s != me)
            def _(s=s):
                q_copy(s, s).wait_recv()

            packed = qall[s]
            pieces += [packed[:, :DH], packed[:, DH:]]
        query = jnp.concatenate(pieces, axis=0)
        memory = kvall[...]
        scores = lax.dot_general(
            query, memory[:, :DH], (((1,), (1,)), ((), ())), preferred_element_type=jnp.float32
        )
        top = jnp.max(scores, axis=1, keepdims=True)
        expo = jnp.exp2((scores - top) * (0.125 * LOG2E))
        total = jnp.sum(expo, axis=1, keepdims=True)
        summed = jnp.dot(expo.astype(jnp.bfloat16), memory, preferred_element_type=jnp.float32)
        out = (summed[:, DH:] / total).astype(jnp.bfloat16)
        for j, s in enumerate(whose):
            low = 2 * j * half
            cpack[s] = jnp.concatenate([out[low : low + half], out[low + half : low + share]], axis=1)

            @pl.when(s != me)
            def _(s=s):
                c_copy(s, me).start()

        @pl.when(i == 1)
        def _():
            sources(steps, pass_x)

        return carry

    lax.fori_loop(0, n // together, attend, 0)
    for k in range(1, layers):
        sources(k, pass_b)
    call[me] = cpack[me]
    others(lambda s: c_copy(s, s).wait_recv())
    for c in range(copies):
        for j in range(HEADS // 2):
            one, two = call[c * HEADS + 2 * j], call[c * HEADS + 2 * j + 1]
            r0, cols = c * share, slice(j * PAIR, (j + 1) * PAIR)
            ctx[r0 : r0 + half, cols] = jnp.concatenate([one[:, :DH], two[:, :DH]], axis=1)
            ctx[r0 + half : r0 + share, cols] = jnp.concatenate([one[:, DH:], two[:, DH:]], axis=1)

    def take_b(z):
        mates = mate % plane
        b_copy(z, 0, mates).wait_recv()
        b_copy(z, 1, mates).wait_recv()

    take_b(zed)
    beyond(take_b)
    width = ow_ref.shape[1]
    for d in range(0, n, 2):
        pair = jnp.concatenate([wall[d], wall[d + 1]], axis=1)
        o_ref[:, d * width : (d + 2) * width] = jnp.dot(
            ctx[...], pair, preferred_element_type=jnp.float32
        ).astype(jnp.bfloat16)

    def sent(d):
        q_copy(d, me).wait_send()
        kv_copy(d, me).wait_send()
        c_copy(d, me).wait_send()

    others(sent)

    def sent_layer(z):
        for p in range(split):
            y_copy(z, spot, over, p).wait_send()
            for g in range(1, groups):
                x_copy(z, 0, g, grp, p).wait_send()
                x_copy(z, 1, g, grp, p).wait_send()
        b_copy(z, 0, spot).wait_send()
        b_copy(z, 1, spot).wait_send()

    beyond(sent_layer)

    def sent_hop(z, carry):
        @pl.when(z <= zed)
        def _():
            for p in range(split):
                hop(z, 0, p, lambda copy: copy.wait_send())

        @pl.when(z >= zed)
        def _():
            for p in range(split):
                hop(z, 1, p, lambda copy: copy.wait_send())

        return carry

    lax.fori_loop(0, layers, sent_hop, 0)
    near_copy(spot, over).wait_send()
    b_copy(zed, 0, spot).wait_send()
    b_copy(zed, 1, spot).wait_send()


def per_device(groups, n, queries, encoder_rows, key_weight, value_weight, out_weight):
    rows = queries.shape[0]
    enc, model = encoder_rows.shape
    wide = key_weight.shape[1]
    depth, width = out_weight.shape
    plane = math.gcd(n, 4)
    layers = n // plane
    chunks = 4
    split = SPLIT
    half = rows // (n // HEADS) // 2
    bf16 = jnp.bfloat16
    dma = lambda k: pltpu.SemaphoreType.DMA((k,))
    vmem = pl.BlockSpec(memory_space=pltpu.VMEM)
    hbm = pl.BlockSpec(memory_space=pl.ANY)
    return pl.pallas_call(
        functools.partial(kernel, groups, n, plane, chunks),
        out_shape=jax.ShapeDtypeStruct((rows, n * width), bf16),
        in_specs=[hbm, hbm, hbm, hbm, hbm],
        out_specs=vmem,
        scratch_shapes=[
            pltpu.VMEM((rows, wide), bf16),
            pltpu.VMEM((enc, model), bf16),
            pltpu.VMEM((chunks, model, wide // chunks), bf16),
            pltpu.VMEM((chunks, model, wide // chunks), bf16),
            pltpu.VMEM((n, half, PAIR), bf16),
            pltpu.VMEM((HEADS, enc, PAIR), bf16),
            pltpu.VMEM((n, half, PAIR), bf16),
            pltpu.VMEM((n * enc, PAIR), bf16),
            pltpu.VMEM((n, half, PAIR), bf16),
            pltpu.VMEM((n, half, PAIR), bf16),
            pltpu.VMEM((rows, depth), bf16),
            pltpu.VMEM((n, depth, width), bf16),
            dma(2 * chunks),
            pltpu.SemaphoreType.DMA,
            dma(2),
            dma(n), dma(n), dma(n), dma(n), dma(n), dma(n),
            dma(2 * layers * split), dma(layers * split), dma(layers * split), dma(layers * split),
            dma(2 * groups * layers * split), dma(2 * groups * layers * split),
            dma(2 * layers), dma(2 * layers),
        ],
        compiler_params=pltpu.CompilerParams(
            collective_id=0, has_side_effects=True, vmem_limit_bytes=60 * 1024 * 1024
        ),
    )(queries, encoder_rows, key_weight, value_weight, out_weight)


def solution(mesh):
    groups, n = mesh.shape["groups"], mesh.shape["ctx"]
    return jax.shard_map(
        functools.partial(per_device, groups, n),
        mesh=mesh,
        in_specs=(P(("groups", "ctx"), None), P(("groups", "ctx"), None), P(), P(), P(None, "ctx")),
        out_specs=P(("groups", "ctx"), None),
        check_vma=False,
    )
```
